32 devices in a mesh: segment: 4 (over y, x), region: 8 (over z, core).
Axes of the slice: x: 2, y: 2, z: 4, core: 2. Of those that a mesh axis runs over, the one named last changes fastest.
Arguments:
- features: bfloat16 [4, 2048, 512], P('segment', 'region'), may hold values from -6 to 6
- edge_weights: bfloat16 [4, 16, 3, 128, 128], P('segment', 'region'), may hold values from -4 to 4
- adjacency: int32 [4, 16, 3], P('segment', 'region'), may hold values from 0 to 3, as said below
- counts: int32 [4, 8], P('segment'), may hold values from 128 to 256, as said below
- weight_self: bfloat16 [4, 512, 512], P('segment'), may hold values from -0.25 to 0.25
- weight_neighbour: bfloat16 [4, 512, 512], P('segment'), may hold values from -0.25 to 0.25
- cotangent: bfloat16 [4, 2048, 512], P('segment', 'region'), may hold values from -6 to 6
Outputs:
- final_hidden: bfloat16 [4, 2048, 512], P('segment', 'region')
- input_grad: bfloat16 [4, 2048, 512], P('segment', 'region')
- grad_self: float32 [4, 512, 512], P('segment')
- grad_neighbour: float32 [4, 512, 512], P('segment')
The draws below stay inside these ranges and needn't reach their ends.
Inputs may be any that keep to these rules, and one draw needn't show every extreme that they name: `adjacency`: each row names 3 distinct extended positions; the row of a block at own position p includes p; the row of a region's first block includes position 0 and that of its last block includes the last extended position. `counts`: in every event some region holds exactly 256 real hits.
All inputs are finite; a program needn't handle non-finite values.
Results may differ from the reference program's by a relative error of at most 0.018.
Values may be sent and summed in bfloat16 or wider, within the bound.
A program may use at most 64 MiB of HBM per device.

```python
import math
import jax
import jax.numpy as jnp
from jax import lax

D = 512
BLK = 128
NNB = 3
HITS_DEV = 256
LAYERS = 4
MB = 4
REGIONS = 8
HITS = 2048


def draw_edge_weights(key, part):
    block_count = HITS_DEV // BLK
    rows_all = REGIONS * block_count
    shape = (MB, rows_all, NNB, BLK, BLK)
    base = jax.random.fold_in(key, 7321)
    key_vals, key_rows, key_cols = jax.random.split(base, 3)
    values = jnp.clip(jax.random.normal(key_vals, shape, jnp.float32), -4.0, 4.0)
    row_log = jax.random.uniform(key_rows, (MB, rows_all, 1, BLK, 1), jnp.float32, math.log(0.1), 0.0)
    col_log = jax.random.uniform(key_cols, (MB, rows_all, NNB, 1, BLK), jnp.float32, math.log(0.1), 0.0)
    return (values * jnp.exp(row_log) * jnp.exp(col_log)).astype(jnp.bfloat16)


def draw_adjacency(key, part):
    block_count = HITS_DEV // BLK
    extent = block_count + 2
    grid_shape = (MB, REGIONS, block_count, extent)
    scores = jax.random.randint(key, grid_shape, 0, 1000)
    position = lax.broadcasted_iota(jnp.int32, grid_shape, 3)
    block_pos = lax.broadcasted_iota(jnp.int32, grid_shape, 2)
    forced = (position == block_pos + 1) | (block_pos == 0) & (position == 0) | (block_pos == block_count - 1) & (position == extent - 1)
    ranked = scores * extent + position + forced.astype(jnp.int32) * 100000000
    picked = lax.top_k(ranked, NNB)[1]
    return picked.reshape(MB, REGIONS * block_count, NNB).astype(jnp.int32)


def draw_counts(key, part):
    key_vals, key_full = jax.random.split(key)
    values = jax.random.randint(key_vals, (MB, REGIONS), HITS_DEV // 2, HITS_DEV + 1)
    fullest = jax.random.randint(key_full, (MB, 1), 0, REGIONS)
    column = lax.broadcasted_iota(jnp.int32, (MB, REGIONS), 1)
    return jnp.where(column == fullest, HITS_DEV, values).astype(jnp.int32)


def block_scale(own_key, shape, pieces, least, top_value):
    level = 1.0
    for axis_at, parts in pieces:
        heights = jax.random.uniform(jax.random.fold_in(jax.random.fold_in(own_key, 6), axis_at), (parts,), jnp.float32, least / len(pieces), top_value / len(pieces))
        level = level * jnp.repeat(jnp.exp(heights), shape[axis_at] // parts).reshape((-1,) + (1,) * (len(shape) - 1 - axis_at))
    return level


def centred(stream_key, shape, width, reach, cuts=(), kind=jnp.bfloat16):
    values = width * jax.random.normal(stream_key, shape, jnp.float32)
    if cuts:
        values = values * block_scale(stream_key, shape, cuts, -0.22, 0.18)
    return jnp.clip(values, -reach, reach).astype(kind)


def setup_inputs(seed: int = 0) -> dict:
    keys = jax.random.split(jax.random.key(seed), 8)
    features = centred(keys[0], (MB, HITS, D), 1.0, 6.0, ((0, 4), (1, 8)))
    edge_weights = draw_edge_weights(jax.random.fold_in(keys[7], 71), 0)
    adjacency = draw_adjacency(jax.random.fold_in(keys[7], 71), 0)
    counts = draw_counts(jax.random.fold_in(keys[7], 71), 0)
    weight_self = centred(keys[4], (LAYERS, D, D), D ** -0.5, 0.25, ((0, 4),))
    weight_neighbour = centred(keys[5], (LAYERS, D, D), D ** -0.5, 0.25, ((0, 4),))
    cotangent = centred(keys[6], (MB, HITS, D), 1.0, 6.0, ((0, 4), (1, 8)))
    return dict(features=features, edge_weights=edge_weights, adjacency=adjacency, counts=counts, weight_self=weight_self, weight_neighbour=weight_neighbour, cotangent=cotangent)


def silu_slope(preact):
    sigmoid_v = jax.nn.sigmoid(preact)
    return sigmoid_v * (1.0 + preact * (1.0 - sigmoid_v))

def extend(block_rows):
    before = jnp.roll(block_rows[:, -1], 1, axis=0)
    after = jnp.roll(block_rows[:, 0], -1, axis=0)
    return jnp.concatenate([before[:, None], block_rows, after[:, None]], axis=1)

def pick_blocks(extended, chosen):
    return jnp.take(extended, chosen, axis=0)

def reference(features, edge_weights, adjacency, counts, weight_self, weight_neighbour, cotangent):
    block_count = HITS_DEV // BLK
    factor = 1.0 / math.sqrt(MB * HITS)
    grad_self = jnp.zeros((LAYERS, D, D), jnp.float32)
    grad_nbr = jnp.zeros((LAYERS, D, D), jnp.float32)
    finals = []
    input_grads = []
    for event_pos in range(MB):
        edge_tiles = edge_weights[event_pos].reshape(REGIONS, block_count, NNB, BLK, BLK)
        tiles_wide = edge_tiles.astype(jnp.float32)
        pattern = adjacency[event_pos].reshape(REGIONS, block_count, NNB)
        squares = lax.optimization_barrier(jnp.sum(jnp.square(tiles_wide), axis=(2, 4)))
        divisor = (1.0 + jnp.sqrt(squares)).reshape(REGIONS, HITS_DEV, 1)
        slot_ids = lax.broadcasted_iota(jnp.int32, (REGIONS, HITS_DEV, 1), 1)
        inside = (slot_ids < counts[event_pos][:, None, None]).astype(jnp.float32)
        hidden = features[event_pos].reshape(REGIONS, HITS_DEV, D)
        hidden = jnp.where(inside > 0, hidden, jnp.zeros_like(hidden))
        saved = []
        for layer_pos in range(LAYERS):
            extended = extend(hidden.reshape(REGIONS, block_count, BLK, D))
            picked = jax.vmap(pick_blocks)(extended, pattern)
            summed = jnp.einsum('rbkij,rbkjd->rbid', tiles_wide, picked.astype(jnp.float32))
            neighbour = (summed.reshape(REGIONS, HITS_DEV, D) / divisor).astype(jnp.bfloat16)
            preact = jnp.dot(hidden.reshape(-1, D), weight_self[layer_pos], preferred_element_type=jnp.float32)
            preact = preact + jnp.dot(neighbour.reshape(-1, D), weight_neighbour[layer_pos], preferred_element_type=jnp.float32)
            preact = preact.reshape(REGIONS, HITS_DEV, D)
            saved.append((hidden, neighbour, preact))
            hidden = (inside * (hidden.astype(jnp.float32) + jax.nn.silu(preact))).astype(jnp.bfloat16)
        finals.append(hidden.reshape(HITS, D))
        gradient = cotangent[event_pos].reshape(REGIONS, HITS_DEV, D)
        for layer_pos in reversed(range(LAYERS)):
            start_h, neighbour, preact = saved[layer_pos]
            masked = inside * gradient.astype(jnp.float32)
            slope_bf = (masked * silu_slope(preact)).astype(jnp.bfloat16)
            slope_flat = slope_bf.reshape(-1, D)
            back_nbr = jnp.dot(slope_flat, weight_neighbour[layer_pos].T, preferred_element_type=jnp.float32)
            scaled = (back_nbr.reshape(REGIONS, HITS_DEV, D) / divisor).astype(jnp.bfloat16)
            scaled = scaled.reshape(REGIONS, block_count, BLK, D)
            spread_back = jnp.einsum('rbkij,rbid->rbkjd', tiles_wide, scaled.astype(jnp.float32))
            ext_ids = lax.broadcasted_iota(jnp.int32, (1, 1, 1, block_count + 2), 3)
            onehot = (pattern[..., None] == ext_ids).astype(jnp.float32)
            ext_grad = jnp.einsum('rbkm,rbkjd->rmjd', onehot, spread_back, precision=lax.Precision.HIGHEST)
            own_grad = ext_grad[:, 1:block_count + 1]
            own_grad = own_grad.at[:, 0].add(jnp.roll(ext_grad[:, block_count + 1], 1, axis=0))
            own_grad = own_grad.at[:, block_count - 1].add(jnp.roll(ext_grad[:, 0], -1, axis=0))
            back_self = jnp.dot(slope_flat, weight_self[layer_pos].T, preferred_element_type=jnp.float32)
            total = masked + back_self.reshape(REGIONS, HITS_DEV, D) + own_grad.reshape(REGIONS, HITS_DEV, D)
            gradient = total.astype(jnp.bfloat16)
            grad_self = grad_self.at[layer_pos].add(jnp.dot(start_h.reshape(-1, D).T, slope_flat, preferred_element_type=jnp.float32))
            grad_nbr = grad_nbr.at[layer_pos].add(jnp.dot(neighbour.reshape(-1, D).T, slope_flat, preferred_element_type=jnp.float32))
        input_grads.append(jnp.where(inside > 0, gradient, jnp.zeros_like(gradient)).reshape(HITS, D))
    return (jnp.stack(finals), jnp.stack(input_grads), grad_self * factor, grad_nbr * factor)
```

```python
import functools
import math

import jax
import jax.numpy as jnp
from jax import lax
from jax.experimental import pallas as pl
from jax.experimental.pallas import tpu as pltpu
from jax.sharding import PartitionSpec as P

BF = jnp.bfloat16
LAG = 1
PARTS = 4
F32 = jnp.float32


def mm(a, b, ca, cb):
    return lax.dot_general(a, b, (((ca,), (cb,)), ((), ())), preferred_element_type=F32)


def kernel(
    S, R, adj, cnt, feat_in, edge_in, ws, wn, cot, final, igrad, gs, gn,
    feat, edge, w, cotv, hn, pre, fh, bs, bh, slope, pact, pslope, gsend, srecv, zs, zrecv, zg, mv, pm,
    a_own, a_halo, inv_ref, mask_ref,
    loc_sem, ww_s, ww_r, wp_s, wp_r, fh_s, fh_r, bh_s, bh_r, pa_s, pa_r, ps_s, ps_r,
    sg_s, sg_r, zr_s, zr_r, zg_s, zg_r, mv_s, mv_r, pm_s, pm_r,
):
    L, Z = S, R // 2
    BLK = edge.shape[-1]
    ROWS, D = feat.shape
    CH = D // S
    Q, DQ = zs.shape[1], D // zs.shape[1]
    pr, pc = zs.shape[3:]
    cols = DQ // pc
    HD = D // 2
    s, r = lax.axis_index("segment"), lax.axis_index("region")
    z, c = r // 2, r % 2
    left, right = (r + R - 1) % R, (r + 1) % R
    partner = r + 1 - 2 * c
    sx, sy = s + 1 - 2 * (s % 2), s + 2 - 4 * (s // 2)

    def rc(src, dst, ss, rs, dev):
        return pltpu.make_async_remote_copy(
            src_ref=src, dst_ref=dst, send_sem=ss, recv_sem=rs,
            device_id=dev, device_id_type=pl.DeviceIdType.MESH,
        )

    pending = []

    def go(cp):
        cp.start()
        pending.append(cp)
        return cp

    own_w = [
        pltpu.make_async_copy(ws, w.at[s, 0], loc_sem.at[0]),
        pltpu.make_async_copy(wn, w.at[s, 1], loc_sem.at[1]),
    ]
    own_cot = pltpu.make_async_copy(cot, cotv, loc_sem.at[2])
    own_feat = pltpu.make_async_copy(feat_in, feat, loc_sem.at[3])
    own_edge = pltpu.make_async_copy(edge_in, edge, loc_sem.at[4])

    barrier = pltpu.get_barrier_semaphore()
    greet = [(s, left), (s, right)]
    greet += [((s + k) % S, r) for k in range(1, S)]
    greet += [(s, (r + 2 * k) % R) for k in range(1, Z)]
    for dev in greet:
        pl.semaphore_signal(barrier, inc=1, device_id=dev, device_id_type=pl.DeviceIdType.MESH)
    for cp in [own_feat] + own_w + [own_edge, own_cot]:
        cp.start()

    limit = cnt[0, r]
    rows = lax.broadcasted_iota(jnp.int32, (ROWS, D), 0)
    mask_ref[...] = (rows < limit).astype(F32)
    mask = lambda: mask_ref[...]
    own_feat.wait()
    h0 = jnp.where(mask() > 0, feat[...], jnp.zeros((ROWS, D), BF))
    hn[0, 0] = h0
    pl.semaphore_wait(barrier, len(greet))

    def halo_send(l):
        go(rc(hn.at[l, 0, pl.ds(ROWS - BLK, BLK)], fh.at[l, pl.ds(0, BLK)],
              fh_s.at[l, 0], fh_r.at[l, 0], (s, right)))
        go(rc(hn.at[l, 0, pl.ds(0, BLK)], fh.at[l, pl.ds(BLK, BLK)],
              fh_s.at[l, 1], fh_r.at[l, 1], (s, left)))

    def halo_wait(l, buf, rs):
        for i in range(2):
            part = buf.at[l, pl.ds(i * BLK, BLK)]
            rc(part, part, rs.at[l, i], rs.at[l, i], (s, left)).wait_recv()

    halo_send(0)
    for cp in own_w:
        cp.wait()

    def half(l, h):
        return w.at[l, c, pl.ds(h * HD, HD)]

    def w_send(h, to, i):
        return rc(half(s, h), half(s, h), ww_s.at[i], ww_r.at[s, h], (to, r))

    first = [w_send(0, sx, 0), w_send(1, sy, 1)]
    second = [w_send(1, sx, 2), w_send(0, sy, 3)]
    for cp in first:
        go(cp)

    @pl.when(s == 0)
    def _():
        for cp in second:
            cp.start()

    own_edge.wait()
    for b in range(2):
        blk = pl.ds(b * BLK, BLK)
        tiles = [edge[b, k] for k in range(3)]
        sq = sum(jnp.sum(jnp.square(t.astype(F32)), axis=1, keepdims=True) for t in tiles)
        inv_ref[blk, :] = jnp.broadcast_to(1.0 / (1.0 + jnp.sqrt(sq)), (BLK, D))
        for m in range(4):
            part = jnp.zeros((BLK, BLK), F32)
            for k in range(3):
                part = jnp.where(adj[b, k] == m, tiles[k].astype(F32), part)
            part = part.astype(BF)
            if m == 0:
                a_halo[blk, pl.ds(0, BLK)] = part
            elif m == 3:
                a_halo[blk, pl.ds(BLK, BLK)] = part
            else:
                a_own[blk, pl.ds((m - 1) * BLK, BLK)] = part

    def w_recv(l, h):
        rc(half(l, h), half(l, h), ww_s.at[0], ww_r.at[l, h], (s, partner)).wait_recv()

    def to_partner(l, h):
        return rc(half(l, h), half(l, h), wp_s.at[l, h], wp_r.at[l, h], (s, partner))

    def relays():
        for l, h, to, i in ((sx, 0, sy, 4), (sy, 1, sx, 5)):
            w_recv(l, h)
            go(rc(half(l, h), half(l, h), ww_s.at[i], ww_r.at[l, h], (to, r)))
            go(to_partner(l, h))

        @pl.when(s != 0)
        def _():
            for cp in second:
                cp.start()

        pending.extend(second)

    def w_forward(l):
        for h in range(2):
            @pl.when((s != l) & ((sx, sy)[h] != l))
            def _():
                w_recv(l, h)
                to_partner(l, h).start()

    def w_wait(l):
        @pl.when(s != l)
        def _():
            for h in range(2):
                src = w.at[l, 1 - c, pl.ds(h * HD, HD)]
                rc(src, src, wp_s.at[l, h], wp_r.at[l, h], (s, partner)).wait_recv()

    for l in range(L):
        own = mm(a_own[...], hn[l, 0], 1, 0)
        if l == 0:
            relays()
            w_forward(0)
            w_wait(0)
        selfp = mm(hn[l, 0], w[l, 0], 1, 0)
        halo_wait(l, fh, fh_r)
        nbr = ((own + mm(a_halo[...], fh[l], 1, 0)) * inv_ref[...]).astype(BF)
        hn[l, 1] = nbr
        p = selfp + mm(nbr, w[l, 1], 1, 0)
        pre[l] = p
        out = hn[l, 0].astype(F32) + p * jax.nn.sigmoid(p)
        nxt = (mask() * out).astype(BF)
        if l + 1 < L:
            hn[l + 1, 0] = nxt
            halo_send(l + 1)
            w_forward(l + 1)
            go(rc(hn.at[l, 1 - c], pact.at[l], pa_s.at[l], pa_r.at[l], (s, partner)))
            w_wait(l + 1)
        else:
            final[...] = nxt
            go(rc(hn.at[l, 1 - c], pact.at[l], pa_s.at[l], pa_r.at[l], (s, partner)))

    def stage_b(l):
        rc(pact.at[l], pact.at[l], pa_s.at[l], pa_r.at[l], (s, partner)).wait_recv()
        rc(pslope.at[l], pslope.at[l], ps_s.at[l], ps_r.at[l], (s, partner)).wait_recv()
        for q in range(Q):
            cs = pl.ds(q * DQ, DQ)
            g = mm(hn[l, c], slope[l, :, cs], 0, 0) + mm(pact[l], pslope[l, :, cs], 0, 0)
            gsend[l, q] = g.reshape(S, CH, DQ).astype(BF)
            for k in range(1, S):
                go(rc(gsend.at[l, q, (s + k) % S], srecv.at[l, q, k - 1],
                      sg_s.at[l, q, k - 1], sg_r.at[l, q, k - 1], ((s + k) % S, r)))

    def stage_c(l, q):
        acc = gsend[l, q, s].astype(F32)
        for k in range(1, S):
            x = srecv.at[l, q, k - 1]
            rc(x, x, sg_s.at[l, q, k - 1], sg_r.at[l, q, k - 1], ((s + k) % S, r)).wait_recv()
            acc = acc + srecv[l, q, k - 1].astype(F32)
        acc = acc.astype(BF)
        for i in range(Z):
            a, b = (i // cols) * pr, (i % cols) * pc
            zs[l, q, i] = acc[a:a + pr, b:b + pc]
        for k in range(1, Z):
            go(rc(zs.at[l, q, (z + k) % Z], zrecv.at[l, q, k - 1],
                  zr_s.at[l, q, k - 1], zr_r.at[l, q, k - 1], (s, (r + 2 * k) % R)))

    def stage_d(l, q):
        acc = zs[l, q, z].astype(F32)
        for k in range(1, Z):
            x = zrecv.at[l, q, k - 1]
            rc(x, x, zr_s.at[l, q, k - 1], zr_r.at[l, q, k - 1], (s, (r + 2 * k) % R)).wait_recv()
            acc = acc + zrecv[l, q, k - 1].astype(F32)
        zg[l, q, z] = acc.astype(BF)
        for k in range(1, Z):
            go(rc(zg.at[l, q, z], zg.at[l, q, z],
                  zg_s.at[l, q, k - 1], zg_r.at[l, q, k - 1], (s, (r + 2 * k) % R)))

    def move(l, q):
        i = (l - s + S) % S
        return rc(zg.at[l, q], mv.at[s, q], mv_s.at[q, i], mv_r.at[q, i], (l, r))

    def stage_e(l, q):
        for k in range(1, Z):
            x = zg.at[l, q, (z + Z - k) % Z]
            rc(x, x, zg_s.at[l, q, k - 1], zg_r.at[l, q, k - 1], (s, (r + 2 * k) % R)).wait_recv()

        @pl.when(s != l)
        def _():
            move(l, q).start()

    def stage(f, l):
        if l < L:
            for q in range(Q):
                f(l, q)

    own_cot.wait()
    grad = cotv[...].astype(F32)
    for l in reversed(range(L)):
        masked = mask() * grad
        p = pre[l]
        sg = jax.nn.sigmoid(p)
        sl = (masked * (sg * (1.0 + p * (1.0 - sg)))).astype(BF)
        slope[l] = sl
        scaled = (mm(sl, w[l, 1], 1, 1) * inv_ref[...]).astype(BF)
        bs[l] = mm(a_halo[...], scaled, 0, 0).astype(BF)
        go(rc(bs.at[l, pl.ds(0, BLK)], bh.at[l, pl.ds(BLK, BLK)],
              bh_s.at[l, 0], bh_r.at[l, 1], (s, left)))
        go(rc(bs.at[l, pl.ds(BLK, BLK)], bh.at[l, pl.ds(0, BLK)],
              bh_s.at[l, 1], bh_r.at[l, 0], (s, right)))
        go(rc(slope.at[l], pslope.at[l], ps_s.at[l], ps_r.at[l], (s, partner)))
        total = masked + mm(sl, w[l, 0], 1, 1) + mm(a_own[...], scaled, 0, 0)
        stage_b(l)
        stage(stage_c, l + LAG)
        stage(stage_d, l + LAG + 1)
        stage(stage_e, l + LAG + 2)
        halo_wait(l, bh, bh_r)
        grad = (total + bh[l].astype(F32)).astype(BF).astype(F32)
    igrad[...] = (mask() * grad).astype(BF)

    for l in range(-1, -LAG - 3, -1):
        for f, m in ((stage_e, l + LAG + 2), (stage_d, l + LAG + 1), (stage_c, l + LAG)):
            if 0 <= m:
                stage(f, m)

    def pair(k, q):
        x = (s + S - k) % S
        return rc(mv.at[x, q], pm.at[x, q], pm_s.at[q, k], pm_r.at[q, k], (s, partner))

    for q in range(Q):
        mv[s, q] = zg[s, q]
        go(pair(0, q))
        for k in range(1, S):
            x = mv.at[(s + S - k) % S, q]
            rc(x, x, mv_s.at[q, k], mv_r.at[q, k], (s, partner)).wait_recv()
            go(pair(k, q))
    for q in range(Q):
        for k in range(S):
            pair(k, q).wait_recv()
    for q in range(Q):
        for k in range(S):
            for i in range(Z):
                a, b = k * CH + (i // cols) * pr, q * DQ + (i % cols) * pc
                mine, other = mv[k, q, i], pm[k, q, i]
                gs[pl.ds(a, pr), pl.ds(b, pc)] = jnp.where(c == 0, mine, other)
                gn[pl.ds(a, pr), pl.ds(b, pc)] = jnp.where(c == 0, other, mine)
    for cp in pending:
        cp.wait_send()
    for l in range(L):
        @pl.when(s != l)
        def _():
            for q in range(Q):
                move(l, q).wait_send()
        for h in range(2):
            @pl.when((s != l) & ((sx, sy)[h] != l))
            def _():
                to_partner(l, h).wait_send()


def emit(scale, final, igrad, gs, gn, final_out, igrad_out, gs_out, gn_out, wide, sem):
    copies = [
        pltpu.make_async_copy(final, final_out.at[0], sem.at[0]),
        pltpu.make_async_copy(igrad, igrad_out.at[0], sem.at[1]),
    ]
    for cp in copies:
        cp.start()
    step = gs.shape[0] // PARTS
    for m, (src, dst) in enumerate(((gs, gs_out), (gn, gn_out))):
        for i in range(PARTS):
            part = pl.ds(i * step, step)
            wide[m, part] = src[part].astype(F32) * scale
            cp = pltpu.make_async_copy(wide.at[m, part], dst.at[0, part], sem.at[2 + m * PARTS + i])
            cp.start()
            copies.append(cp)
    for cp in copies:
        cp.wait()


def body(features, edge_weights, adjacency, counts, weight_self, weight_neighbour, cotangent):
    R, S = lax.axis_size("region"), lax.axis_size("segment")
    rows, D = features.shape[1:]
    blk = edge_weights.shape[3]
    L, Z, CH = S, R // 2, D // S
    Q = 2 if Z <= CH // 16 else 1
    rg = min(Z, CH // 16)
    cg = Z // rg
    pr, pc = CH // rg, D // Q // cg
    scale = 1.0 / math.sqrt(S * features.shape[0] * rows * R)
    V = pltpu.VMEM
    DMA = pltpu.SemaphoreType.DMA
    vm = pl.BlockSpec(memory_space=pltpu.VMEM)
    sm = pl.BlockSpec(memory_space=pltpu.SMEM)
    anys = pl.BlockSpec(memory_space=pl.ANY)
    sems = [DMA((5,))]
    for shape in [((6,), (L, 2)), ((L, 2),) * 2, ((L, 2),) * 2, ((L, 2),) * 2, ((L,),) * 2, ((L,),) * 2,
                  ((L, Q, S - 1),) * 2, ((L, Q, Z - 1),) * 2, ((L, Q, Z - 1),) * 2, ((Q, S),) * 2, ((Q, S),) * 2]:
        sems += [DMA(shape[0]), DMA(shape[1])]
    final, igrad, gs, gn = pl.pallas_call(
        functools.partial(kernel, S, R),
        out_shape=(
            V((rows, D), BF), V((rows, D), BF), V((D, D), BF), V((D, D), BF),
        ),
        in_specs=[sm, sm, anys, anys, anys, anys, anys],
        out_specs=(vm, vm, vm, vm),
        scratch_shapes=[
            V((rows, D), BF), V(edge_weights.shape[1:], BF), V((S, 2, D, D), BF), V((rows, D), BF), V((L, 2, rows, D), BF), V((L, rows, D), F32),
            V((L, 2 * blk, D), BF), V((L, 2 * blk, D), BF), V((L, 2 * blk, D), BF),
            V((L, rows, D), BF), V((L, rows, D), BF), V((L, rows, D), BF),
            V((L, Q, S, CH, D // Q), BF), V((L, Q, S - 1, CH, D // Q), BF),
            V((L, Q, Z, pr, pc), BF), V((L, Q, Z - 1, pr, pc), BF), V((L, Q, Z, pr, pc), BF),
            V((S, Q, Z, pr, pc), BF), V((S, Q, Z, pr, pc), BF),
            V((rows, 2 * blk), BF), V((rows, 2 * blk), BF), V((rows, D), F32), V((rows, D), F32),
        ] + sems,
        compiler_params=pltpu.CompilerParams(
            collective_id=0, has_side_effects=True, vmem_limit_bytes=60 * 1024 * 1024
        ),
        name="network",
    )(adjacency[0], counts, features[0], edge_weights[0], weight_self[0], weight_neighbour[0], cotangent[0])
    outs = pl.pallas_call(
        functools.partial(emit, scale),
        out_shape=(
            jax.ShapeDtypeStruct((1, rows, D), BF),
            jax.ShapeDtypeStruct((1, rows, D), BF),
            jax.ShapeDtypeStruct((1, D, D), F32),
            jax.ShapeDtypeStruct((1, D, D), F32),
        ),
        in_specs=[vm] * 4,
        out_specs=(anys,) * 4,
        scratch_shapes=[V((2, D, D), F32), DMA((2 + 2 * PARTS,))],
        compiler_params=pltpu.CompilerParams(vmem_limit_bytes=8 * 1024 * 1024),
        name="emit",
    )(final, igrad, gs, gn)
    return tuple(outs)


def solution(mesh):
    in_specs = (
        P("segment", "region", None),
        P("segment", "region", None, None, None),
        P("segment", "region", None),
        P("segment", None),
        P("segment", None, None),
        P("segment", None, None),
        P("segment", "region", None),
    )
    out_specs = (
        P("segment", "region", None),
        P("segment", "region", None),
        P("segment", None, None),
        P("segment", None, None),
    )
    return jax.shard_map(body, mesh=mesh, in_specs=in_specs, out_specs=out_specs, check_vma=False)
```

```python
import functools
import math

import jax
import jax.numpy as jnp
from jax import lax
from jax.experimental import pallas as pl
from jax.experimental.pallas import tpu as pltpu
from jax.sharding import PartitionSpec as P

BF = jnp.bfloat16
PLAN = ((0, 1), (1, 2), (2, 3), (3, 4))
PARTS = 4
F32 = jnp.float32


def mm(a, b, ca, cb):
    return lax.dot_general(a, b, (((ca,), (cb,)), ((), ())), preferred_element_type=F32)


def kernel(
    S, R, adj, cnt, feat_in, edge_in, ws, wn, cot, final, igrad, gs, gn,
    feat, edge, w, cotv, hn, pre, fh, bs, bh, slope, pact, pslope, gsend, srecv, zs, zrecv, zg, mv, pm,
    a_own, a_halo, inv_ref, mask_ref,
    loc_sem, ww_s, ww_r, wp_s, wp_r, fh_s, fh_r, bh_s, bh_r, pa_s, pa_r, ps_s, ps_r,
    sg_s, sg_r, zr_s, zr_r, zg_s, zg_r, mv_s, mv_r, pm_s, pm_r,
):
    L, Z = S, R // 2
    BLK = edge.shape[-1]
    ROWS, D = feat.shape
    CH = D // S
    Q, DQ = zs.shape[1], D // zs.shape[1]
    tree = Z == 4
    pr, pc = zs.shape[-2:]
    cols = DQ // pc
    HD = D // 2
    s, r = lax.axis_index("segment"), lax.axis_index("region")
    z, c = r // 2, r % 2
    left, right = (r + R - 1) % R, (r + 1) % R
    partner = r + 1 - 2 * c
    sx, sy = s + 1 - 2 * (s % 2), s + 2 - 4 * (s // 2)

    def rc(src, dst, ss, rs, dev):
        return pltpu.make_async_remote_copy(
            src_ref=src, dst_ref=dst, send_sem=ss, recv_sem=rs,
            device_id=dev, device_id_type=pl.DeviceIdType.MESH,
        )

    pending = []

    def go(cp):
        cp.start()
        pending.append(cp)
        return cp

    own_w = [
        pltpu.make_async_copy(ws, w.at[s, 0], loc_sem.at[0]),
        pltpu.make_async_copy(wn, w.at[s, 1], loc_sem.at[1]),
    ]
    own_cot = pltpu.make_async_copy(cot, cotv, loc_sem.at[2])
    own_feat = pltpu.make_async_copy(feat_in, feat, loc_sem.at[3])
    own_edge = pltpu.make_async_copy(edge_in, edge, loc_sem.at[4])

    barrier = pltpu.get_barrier_semaphore()
    greet = [(s, left), (s, right)]
    greet += [((s + k) % S, r) for k in range(1, S)]
    greet += [(s, (r + 2 * k) % R) for k in range(1, Z)]
    for dev in greet:
        pl.semaphore_signal(barrier, inc=1, device_id=dev, device_id_type=pl.DeviceIdType.MESH)
    for cp in [own_feat] + own_w + [own_edge, own_cot]:
        cp.start()

    limit = cnt[0, r]
    rows = lax.broadcasted_iota(jnp.int32, (ROWS, D), 0)
    mask_ref[...] = (rows < limit).astype(F32)
    mask = lambda: mask_ref[...]
    own_feat.wait()
    h0 = jnp.where(mask() > 0, feat[...], jnp.zeros((ROWS, D), BF))
    hn[0, 0] = h0
    pl.semaphore_wait(barrier, len(greet))

    def halo_send(l):
        go(rc(hn.at[l, 0, pl.ds(ROWS - BLK, BLK)], fh.at[l, pl.ds(0, BLK)],
              fh_s.at[l, 0], fh_r.at[l, 0], (s, right)))
        go(rc(hn.at[l, 0, pl.ds(0, BLK)], fh.at[l, pl.ds(BLK, BLK)],
              fh_s.at[l, 1], fh_r.at[l, 1], (s, left)))

    def halo_wait(l, buf, rs):
        for i in range(2):
            part = buf.at[l, pl.ds(i * BLK, BLK)]
            rc(part, part, rs.at[l, i], rs.at[l, i], (s, left)).wait_recv()

    halo_send(0)
    for cp in own_w:
        cp.wait()

    def half(l, h):
        return w.at[l, c, pl.ds(h * HD, HD)]

    def w_send(h, to, i):
        return rc(half(s, h), half(s, h), ww_s.at[i], ww_r.at[s, h], (to, r))

    first = [w_send(0, sx, 0), w_send(1, sy, 1)]
    second = [w_send(1, sx, 2), w_send(0, sy, 3)]
    for cp in first:
        go(cp)

    @pl.when(s == 0)
    def _():
        for cp in second:
            cp.start()

    own_edge.wait()
    for b in range(2):
        blk = pl.ds(b * BLK, BLK)
        tiles = [edge[b, k] for k in range(3)]
        sq = sum(jnp.sum(jnp.square(t.astype(F32)), axis=1, keepdims=True) for t in tiles)
        inv_ref[blk, :] = jnp.broadcast_to(1.0 / (1.0 + jnp.sqrt(sq)), (BLK, D))
        for m in range(4):
            part = jnp.zeros((BLK, BLK), F32)
            for k in range(3):
                part = jnp.where(adj[b, k] == m, tiles[k].astype(F32), part)
            part = part.astype(BF)
            if m == 0:
                a_halo[blk, pl.ds(0, BLK)] = part
            elif m == 3:
                a_halo[blk, pl.ds(BLK, BLK)] = part
            else:
                a_own[blk, pl.ds((m - 1) * BLK, BLK)] = part

    def w_recv(l, h):
        rc(half(l, h), half(l, h), ww_s.at[0], ww_r.at[l, h], (s, partner)).wait_recv()

    def to_partner(l, h):
        return rc(half(l, h), half(l, h), wp_s.at[l, h], wp_r.at[l, h], (s, partner))

    def relays():
        for l, h, to, i in ((sx, 0, sy, 4), (sy, 1, sx, 5)):
            w_recv(l, h)
            go(rc(half(l, h), half(l, h), ww_s.at[i], ww_r.at[l, h], (to, r)))
            go(to_partner(l, h))

        @pl.when(s != 0)
        def _():
            for cp in second:
                cp.start()

        pending.extend(second)

    def w_forward(l):
        for h in range(2):
            @pl.when((s != l) & ((sx, sy)[h] != l))
            def _():
                w_recv(l, h)
                to_partner(l, h).start()

    def w_wait(l):
        @pl.when(s != l)
        def _():
            for h in range(2):
                src = w.at[l, 1 - c, pl.ds(h * HD, HD)]
                rc(src, src, wp_s.at[l, h], wp_r.at[l, h], (s, partner)).wait_recv()

    for l in range(L):
        own = mm(a_own[...], hn[l, 0], 1, 0)
        if l == 0:
            relays()
            w_forward(0)
            w_wait(0)
        selfp = mm(hn[l, 0], w[l, 0], 1, 0)
        halo_wait(l, fh, fh_r)
        nbr = ((own + mm(a_halo[...], fh[l], 1, 0)) * inv_ref[...]).astype(BF)
        hn[l, 1] = nbr
        p = selfp + mm(nbr, w[l, 1], 1, 0)
        pre[l] = p
        out = hn[l, 0].astype(F32) + p * jax.nn.sigmoid(p)
        nxt = (mask() * out).astype(BF)
        if l + 1 < L:
            hn[l + 1, 0] = nxt
            halo_send(l + 1)
            w_forward(l + 1)
            go(rc(hn.at[l, 1 - c], pact.at[l], pa_s.at[l], pa_r.at[l], (s, partner)))
            w_wait(l + 1)
        else:
            final[...] = nxt
            go(rc(hn.at[l, 1 - c], pact.at[l], pa_s.at[l], pa_r.at[l], (s, partner)))

    def stage_b(l):
        rc(pact.at[l], pact.at[l], pa_s.at[l], pa_r.at[l], (s, partner)).wait_recv()
        rc(pslope.at[l], pslope.at[l], ps_s.at[l], ps_r.at[l], (s, partner)).wait_recv()
        for q in range(Q):
            cs = pl.ds(q * DQ, DQ)
            g = mm(hn[l, c], slope[l, :, cs], 0, 0) + mm(pact[l], pslope[l, :, cs], 0, 0)
            gsend[l, q] = g.reshape(S, CH, DQ).astype(BF)
            for k in range(1, S):
                go(rc(gsend.at[l, q, (s + k) % S], srecv.at[l, q, k - 1],
                      sg_s.at[l, q, k - 1], sg_r.at[l, q, k - 1], ((s + k) % S, r)))

    end = (z == 0) | (z == Z - 1)
    inner = jnp.where(z < 2, 1, 2)
    outer = jnp.where(z < 2, 0, 3)

    def to_mid(l, q):
        return rc(zs.at[l, q], zrecv.at[l, q, 0], zr_s.at[l, q, 0], zr_r.at[l, q, 0], (s, 2 * inner + c))

    def across(l, q):
        return rc(zs.at[l, q], zrecv.at[l, q, 1], zr_s.at[l, q, 1], zr_r.at[l, q, 1], (s, 2 * (3 - inner) + c))

    def to_end(l, q):
        return rc(zg.at[l, q], zg.at[l, q], zg_s.at[l, q, 0], zg_r.at[l, q, 0], (s, 2 * outer + c))

    def stage_c(l, q):
        acc = gsend[l, q, s].astype(F32)
        for k in range(1, S):
            x = srecv.at[l, q, k - 1]
            rc(x, x, sg_s.at[l, q, k - 1], sg_r.at[l, q, k - 1], ((s + k) % S, r)).wait_recv()
            acc = acc + srecv[l, q, k - 1].astype(F32)
        if tree:
            zs[l, q] = acc.astype(BF)

            @pl.when(end)
            def _():
                to_mid(l, q).start()

            return
        acc = acc.astype(BF)
        for i in range(Z):
            a, b = (i // cols) * pr, (i % cols) * pc
            zs[l, q, i] = acc[a:a + pr, b:b + pc]
        for k in range(1, Z):
            go(rc(zs.at[l, q, (z + k) % Z], zrecv.at[l, q, k - 1],
                  zr_s.at[l, q, k - 1], zr_r.at[l, q, k - 1], (s, (r + 2 * k) % R)))

    def stage_d(l, q):
        if tree:
            @pl.when(jnp.logical_not(end))
            def _():
                to_mid(l, q).wait_recv()
                zs[l, q] = (zs[l, q].astype(F32) + zrecv[l, q, 0].astype(F32)).astype(BF)
                across(l, q).start()

            return
        acc = zs[l, q, z].astype(F32)
        for k in range(1, Z):
            x = zrecv.at[l, q, k - 1]
            rc(x, x, zr_s.at[l, q, k - 1], zr_r.at[l, q, k - 1], (s, (r + 2 * k) % R)).wait_recv()
            acc = acc + zrecv[l, q, k - 1].astype(F32)
        zg[l, q, z] = acc.astype(BF)
        for k in range(1, Z):
            go(rc(zg.at[l, q, z], zg.at[l, q, z],
                  zg_s.at[l, q, k - 1], zg_r.at[l, q, k - 1], (s, (r + 2 * k) % R)))

    def move(l, q):
        i = (l - s + S) % S
        return rc(zg.at[l, q], mv.at[s, q], mv_s.at[q, i], mv_r.at[q, i], (l, r))

    def stage_e(l, q):
        if tree:
            @pl.when(jnp.logical_not(end))
            def _():
                across(l, q).wait_recv()
                zg[l, q] = (zs[l, q].astype(F32) + zrecv[l, q, 1].astype(F32)).astype(BF)
                to_end(l, q).start()

                @pl.when(s != l)
                def _():
                    move(l, q).start()

            return
        for k in range(1, Z):
            x = zg.at[l, q, (z + Z - k) % Z]
            rc(x, x, zg_s.at[l, q, k - 1], zg_r.at[l, q, k - 1], (s, (r + 2 * k) % R)).wait_recv()

        @pl.when(s != l)
        def _():
            move(l, q).start()

    def stage_f(l, q):
        if tree:
            @pl.when(end)
            def _():
                to_end(l, q).wait_recv()

                @pl.when(s != l)
                def _():
                    move(l, q).start()

    def stage(f, l):
        if l < L:
            for q in range(Q):
                f(l, q)

    own_cot.wait()
    grad = cotv[...].astype(F32)
    for l in reversed(range(L)):
        masked = mask() * grad
        p = pre[l]
        sg = jax.nn.sigmoid(p)
        sl = (masked * (sg * (1.0 + p * (1.0 - sg)))).astype(BF)
        slope[l] = sl
        scaled = (mm(sl, w[l, 1], 1, 1) * inv_ref[...]).astype(BF)
        bs[l] = mm(a_halo[...], scaled, 0, 0).astype(BF)
        go(rc(bs.at[l, pl.ds(0, BLK)], bh.at[l, pl.ds(BLK, BLK)],
              bh_s.at[l, 0], bh_r.at[l, 1], (s, left)))
        go(rc(bs.at[l, pl.ds(BLK, BLK)], bh.at[l, pl.ds(0, BLK)],
              bh_s.at[l, 1], bh_r.at[l, 0], (s, right)))
        go(rc(slope.at[l], pslope.at[l], ps_s.at[l], ps_r.at[l], (s, partner)))
        total = masked + mm(sl, w[l, 0], 1, 1) + mm(a_own[...], scaled, 0, 0)
        stage_b(l)
        for f, lag in PLAN:
            stage((stage_c, stage_d, stage_e, stage_f)[f], l + lag)
        halo_wait(l, bh, bh_r)
        grad = (total + bh[l].astype(F32)).astype(BF).astype(F32)
    igrad[...] = (mask() * grad).astype(BF)

    lags = dict(PLAN)
    for l in range(-1, -1 - max(lags.values()), -1):
        for f, lag in reversed(PLAN):
            if l + lag >= 0:
                stage((stage_c, stage_d, stage_e, stage_f)[f], l + lag)

    def pair(k, q):
        x = (s + S - k) % S
        return rc(mv.at[x, q], pm.at[x, q], pm_s.at[q, k], pm_r.at[q, k], (s, partner))

    for q in range(Q):
        mv[s, q] = zg[s, q]
        go(pair(0, q))
        for k in range(1, S):
            x = mv.at[(s + S - k) % S, q]
            rc(x, x, mv_s.at[q, k], mv_r.at[q, k], (s, partner)).wait_recv()
            go(pair(k, q))
    for q in range(Q):
        for k in range(S):
            pair(k, q).wait_recv()
    for q in range(Q):
        for k in range(S):
            for i in range(1 if tree else Z):
                a, b = k * CH + (i // cols) * pr, q * DQ + (i % cols) * pc
                mine, other = (mv[k, q], pm[k, q]) if tree else (mv[k, q, i], pm[k, q, i])
                gs[pl.ds(a, pr), pl.ds(b, pc)] = jnp.where(c == 0, mine, other)
                gn[pl.ds(a, pr), pl.ds(b, pc)] = jnp.where(c == 0, other, mine)
    for cp in pending:
        cp.wait_send()
    if tree:
        @pl.when(end)
        def _():
            for l in range(L):
                for q in range(Q):
                    to_mid(l, q).wait_send()

        @pl.when(jnp.logical_not(end))
        def _():
            for l in range(L):
                for q in range(Q):
                    across(l, q).wait_send()
                    to_end(l, q).wait_send()

    for l in range(L):
        @pl.when(s != l)
        def _():
            for q in range(Q):
                move(l, q).wait_send()
        for h in range(2):
            @pl.when((s != l) & ((sx, sy)[h] != l))
            def _():
                to_partner(l, h).wait_send()


def emit(scale, final, igrad, gs, gn, final_out, igrad_out, gs_out, gn_out, wide, sem):
    copies = [
        pltpu.make_async_copy(final, final_out.at[0], sem.at[0]),
        pltpu.make_async_copy(igrad, igrad_out.at[0], sem.at[1]),
    ]
    for cp in copies:
        cp.start()
    step = gs.shape[0] // PARTS
    for m, (src, dst) in enumerate(((gs, gs_out), (gn, gn_out))):
        for i in range(PARTS):
            part = pl.ds(i * step, step)
            wide[m, part] = src[part].astype(F32) * scale
            cp = pltpu.make_async_copy(wide.at[m, part], dst.at[0, part], sem.at[2 + m * PARTS + i])
            cp.start()
            copies.append(cp)
    for cp in copies:
        cp.wait()


def body(features, edge_weights, adjacency, counts, weight_self, weight_neighbour, cotangent):
    R, S = lax.axis_size("region"), lax.axis_size("segment")
    rows, D = features.shape[1:]
    blk = edge_weights.shape[3]
    L, Z, CH = S, R // 2, D // S
    Q = 2 if Z <= CH // 16 else 1
    rg = min(Z, CH // 16)
    cg = Z // rg
    pr, pc = CH // rg, D // Q // cg
    piece, got = ((CH, D // Q), (2, CH, D // Q)) if Z == 4 else ((Z, pr, pc), (Z - 1, pr, pc))
    scale = 1.0 / math.sqrt(S * features.shape[0] * rows * R)
    V = pltpu.VMEM
    DMA = pltpu.SemaphoreType.DMA
    vm = pl.BlockSpec(memory_space=pltpu.VMEM)
    sm = pl.BlockSpec(memory_space=pltpu.SMEM)
    anys = pl.BlockSpec(memory_space=pl.ANY)
    sems = [DMA((5,))]
    for shape in [((6,), (L, 2)), ((L, 2),) * 2, ((L, 2),) * 2, ((L, 2),) * 2, ((L,),) * 2, ((L,),) * 2,
                  ((L, Q, S - 1),) * 2, ((L, Q, Z - 1),) * 2, ((L, Q, Z - 1),) * 2, ((Q, S),) * 2, ((Q, S),) * 2]:
        sems += [DMA(shape[0]), DMA(shape[1])]
    final, igrad, gs, gn = pl.pallas_call(
        functools.partial(kernel, S, R),
        out_shape=(
            V((rows, D), BF), V((rows, D), BF), V((D, D), BF), V((D, D), BF),
        ),
        in_specs=[sm, sm, anys, anys, anys, anys, anys],
        out_specs=(vm, vm, vm, vm),
        scratch_shapes=[
            V((rows, D), BF), V(edge_weights.shape[1:], BF), V((S, 2, D, D), BF), V((rows, D), BF), V((L, 2, rows, D), BF), V((L, rows, D), F32),
            V((L, 2 * blk, D), BF), V((L, 2 * blk, D), BF), V((L, 2 * blk, D), BF),
            V((L, rows, D), BF), V((L, rows, D), BF), V((L, rows, D), BF),
            V((L, Q, S, CH, D // Q), BF), V((L, Q, S - 1, CH, D // Q), BF),
            V((L, Q, *piece), BF), V((L, Q, *got), BF), V((L, Q, *piece), BF),
            V((S, Q, *piece), BF), V((S, Q, *piece), BF),
            V((rows, 2 * blk), BF), V((rows, 2 * blk), BF), V((rows, D), F32), V((rows, D), F32),
        ] + sems,
        compiler_params=pltpu.CompilerParams(
            collective_id=0, has_side_effects=True, vmem_limit_bytes=60 * 1024 * 1024
        ),
        name="network",
    )(adjacency[0], counts, features[0], edge_weights[0], weight_self[0], weight_neighbour[0], cotangent[0])
    outs = pl.pallas_call(
        functools.partial(emit, scale),
        out_shape=(
            jax.ShapeDtypeStruct((1, rows, D), BF),
            jax.ShapeDtypeStruct((1, rows, D), BF),
            jax.ShapeDtypeStruct((1, D, D), F32),
            jax.ShapeDtypeStruct((1, D, D), F32),
        ),
        in_specs=[vm] * 4,
        out_specs=(anys,) * 4,
        scratch_shapes=[V((2, D, D), F32), DMA((2 + 2 * PARTS,))],
        compiler_params=pltpu.CompilerParams(vmem_limit_bytes=8 * 1024 * 1024),
        name="emit",
    )(final, igrad, gs, gn)
    return tuple(outs)


def solution(mesh):
    in_specs = (
        P("segment", "region", None),
        P("segment", "region", None, None, None),
        P("segment", "region", None),
        P("segment", None),
        P("segment", None, None),
        P("segment", None, None),
        P("segment", "region", None),
    )
    out_specs = (
        P("segment", "region", None),
        P("segment", "region", None),
        P("segment", None, None),
        P("segment", None, None),
    )
    return jax.shard_map(body, mesh=mesh, in_specs=in_specs, out_specs=out_specs, check_vma=False)
```
